32 devices in a mesh: dp: 2 (over x), expert: 8 (over z, y), tensor: 2 (over core).
Axes of the slice: x: 2, y: 2, z: 4, core: 2. Of those that a mesh axis runs over, the one named last changes fastest.
Arguments:
- tokens: bfloat16 [1024, 4096], P('expert'), may hold values from -6 to 6
- norm_gain: float32 [4096], replicated, may hold values from 0.5 to 1.5
- expert_ids: int32 [1024, 2], P('expert'), may hold values from 0 to 3, all different within a row; in each aligned block of 128 rows (0 to 127, 128 to 255, ...) at most 65 rows name the same one
- gate_values: float32 [1024, 2], P('expert'), may hold values from 0.1 to 1
- gate_weight: bfloat16 [8, 4096, 7168], P('expert', None, ('dp', 'tensor')), may hold values from -0.09375 to 0.09375
- up_weight: bfloat16 [8, 4096, 7168], P('expert', None, ('dp', 'tensor')), may hold values from -0.09375 to 0.09375
- down_weight: bfloat16 [8, 7168, 4096], P('expert', ('dp', 'tensor')), may hold values from -0.046875 to 0.046875
Outputs:
- layer_out: bfloat16 [1024, 4096], P('expert')
The draws below stay inside these ranges and needn't reach their ends.
Inputs may be any that keep to these rules, and one draw needn't show every extreme that they name: `expert_ids`: each row names two different experts. Among the 128 rows of one block no expert is named more than 65 times, and in some such blocks one expert is named exactly 65 times.
All inputs are finite; a program needn't handle non-finite values.
Results may differ from the reference program's by a relative error of at most 0.0095.
Values may be sent and summed in bfloat16 or wider, within the bound.
No kernel may reach another device: no remote copies, remote signals or barrier semaphores. Data moves between devices by JAX's collectives and lax.ppermute only.
A program may use at most 128 MiB of HBM per device.

```python
import math
import jax
import jax.numpy as jnp
import numpy as np
from jax import lax

D = 4096
FF = 14336
TOK_DEV = 128
E = 4
CAPACITY = 65
TOKENS = 1024
N_DP = 2
N_EXPERT = 8
N_TENSOR = 2


def steps_of(rng, extent, pieces, least, top_value):
    def one(position, blocks):
        steps = jax.random.uniform(jax.random.fold_in(jax.random.fold_in(rng, 6), position), (blocks,), jnp.float32, least / len(pieces), top_value / len(pieces))
        return jnp.repeat(jnp.exp(steps), extent[position] // blocks).reshape((-1,) + (1,) * (len(extent) - position - 1))

    loudness = one(*pieces[0])
    for cut in pieces[1:]:
        loudness = loudness * one(*cut)
    return loudness


def shared_out(stream_key, own, number, rows, amount, top, most, skew):
    ranking = jax.random.permutation(stream_key, amount)
    crowded, common = portions_of(amount, rows * top, most, skew, True), portions_of(amount, rows * top, most, skew, False)
    places = jnp.arange(amount)

    def named(sizes, turn):
        used = int((sizes > 0).sum())
        fixed = max(1, used // 4)
        passed = fixed + (places - fixed + turn * (used - fixed)) % max(1, amount - fixed)
        return jnp.zeros((amount,), jnp.int32).at[ranking[jnp.where(places < fixed, places, passed)]].set(jnp.asarray(sizes, jnp.int32))

    sizes = jnp.where(number % 4 == 0, named(crowded, number // 4), named(common, number - number // 4 - 1))
    mixed = jax.random.permutation(jax.random.fold_in(own, 3), amount)
    giver, sink = mixed[0:amount // 2 * 2:2], mixed[1:amount // 2 * 2:2]
    margin = jnp.minimum(sizes[giver] - 1, most - sizes[sink]) // 2
    margin = jnp.where((giver == ranking[0]) | (sink == ranking[0]) | (sizes[sink] == 0), 0, jnp.maximum(margin, 0))
    passed = jax.random.randint(jax.random.fold_in(own, 4), (amount // 2,), 0, 1 << 20) % (margin + 1)
    sizes = sizes.at[giver].add(-passed).at[sink].add(passed)
    items = jnp.searchsorted(jnp.cumsum(sizes), jnp.arange(rows * top), side="right").astype(jnp.int32)
    listing = items.reshape(top, rows).T
    listing = listing[jax.random.permutation(jax.random.fold_in(own, 1), rows)]
    turn = jax.random.randint(jax.random.fold_in(own, 2), (rows, 1), 0, top)
    return jnp.take_along_axis(listing, (jnp.arange(top)[None, :] + turn) % top, axis=1)


def portions_of(number_of, total, reach, slope, full):
    portions = [(1 << 20) // math.isqrt(rank ** slope) + 1 for rank in range(1, number_of + 1)]
    largest = reach if full else min(reach, max(-(-total // number_of), total * portions[0] // sum(portions)))
    least = 1 if total - largest >= number_of - 1 else 0
    given, spare = [largest] + [least] * (number_of - 1), total - largest - least * (number_of - 1)
    while spare > 0:
        movable = [i for i in range(1, number_of) if given[i] < largest] or [i for i in range(1, number_of) if given[i] < reach]
        mass, remaining = sum([portions[i] for i in movable]), spare
        for i in movable:
            extra = min(reach - given[i], max(1, remaining * portions[i] // mass), spare)
            given[i] = given[i] + extra
            spare = spare - extra
    return np.array(given)


def gaussian(key, dims, spread, limit, cuts=(), kind=jnp.bfloat16):
    gain = steps_of(key, dims, cuts, -0.22, 0.18) if cuts else 1.0
    entries = jax.random.normal(key, dims, jnp.float32) * spread * gain
    return jnp.minimum(jnp.maximum(entries, -limit), limit).astype(kind)


def setup_inputs(seed: int = 0) -> dict:
    seeds = jax.random.split(jax.random.key(seed), 8)
    tokens = gaussian(seeds[0], (TOKENS, D), 1.0, 6.0, ((0, 8),))
    norm_gain = jnp.clip(1.0 + 0.1 * jax.random.normal(seeds[1], (D,), jnp.float32), 0.5, 1.5)
    expert_ids_keys = jax.random.split(jax.random.fold_in(seeds[2], 1), TOKENS // TOK_DEV)
    expert_ids_turns = jax.random.permutation(jax.random.fold_in(seeds[2], 3), TOKENS // TOK_DEV)
    expert_ids = jax.vmap(lambda own, number: shared_out(jax.random.fold_in(seeds[2], 2), own, number, TOK_DEV, E, 2, CAPACITY, 1))(expert_ids_keys, expert_ids_turns).reshape((TOKENS, 2))
    gate_values = jnp.clip(0.1 + 0.9 * jax.random.uniform(seeds[3], (TOKENS, 2), jnp.float32) ** steps_of(seeds[3], (TOKENS, 2), ((0, 8),), -0.2, 0.2), 0.1, 1.0)
    gate_weight = gaussian(seeds[4], (2 * E, D, FF // 2), D ** -0.5, 0.09375, ((0, 8), (2, 4)))
    up_weight = gaussian(seeds[5], (2 * E, D, FF // 2), D ** -0.5, 0.09375, ((0, 8), (2, 4)))
    down_weight = gaussian(seeds[6], (2 * E, FF // 2, D), FF ** -0.5, 0.046875, ((0, 8), (1, 4)))
    return {"tokens": tokens, "norm_gain": norm_gain, "expert_ids": expert_ids, "gate_values": gate_values, "gate_weight": gate_weight, "up_weight": up_weight, "down_weight": down_weight}


def reference(tokens, norm_gain, expert_ids, gate_values, gate_weight, up_weight, down_weight):
    inputs = tokens.astype(jnp.float32)
    mean_square = lax.optimization_barrier(jnp.mean(inputs * inputs, axis=-1, keepdims=True))
    normed = (inputs * lax.rsqrt(mean_square + 1e-05) * norm_gain).astype(jnp.bfloat16)
    flat_routes = expert_ids.reshape(N_EXPERT, 2 * TOK_DEV)
    one_hot = (flat_routes[..., None] == jnp.arange(E, dtype=jnp.int32)).astype(jnp.int32)
    prior_count = jnp.cumsum(one_hot, axis=1) - one_hot
    slot_index = lax.optimization_barrier(jnp.sum(prior_count * one_hot, axis=-1)).astype(jnp.int32)
    block_ids = jnp.arange(N_EXPERT, dtype=jnp.int32)[:, None]
    row_index = ((flat_routes * N_EXPERT + block_ids) * CAPACITY + slot_index).reshape(-1).astype(jnp.int32)
    repeated = jnp.repeat(normed, 2, axis=0)
    buffers = jnp.zeros((E * N_EXPERT * CAPACITY, D), jnp.bfloat16).at[row_index].set(repeated)
    buffers = buffers.reshape(E, N_EXPERT * CAPACITY, D)
    group_width = FF // (2 * N_DP * N_TENSOR)
    group_count = N_DP * N_TENSOR

    def run_expert(operands):
        expert_rows, expert_id = operands
        total = jnp.zeros((N_EXPERT * CAPACITY, D), jnp.float32)
        for half_id in range(2):
            index = (2 * expert_id + half_id).astype(jnp.int32)
            gate_half = lax.dynamic_index_in_dim(gate_weight, index, 0, keepdims=False)
            up_half = lax.dynamic_index_in_dim(up_weight, index, 0, keepdims=False)
            down_half = lax.dynamic_index_in_dim(down_weight, index, 0, keepdims=False)

            def group_step(accum, group_id):
                offset = (group_id * group_width).astype(jnp.int32)
                gate_block = lax.dynamic_slice_in_dim(gate_half, offset, group_width, 1)
                up_block = lax.dynamic_slice_in_dim(up_half, offset, group_width, 1)
                down_block = lax.dynamic_slice_in_dim(down_half, offset, group_width, 0)
                gate_part = jnp.dot(expert_rows, gate_block, preferred_element_type=jnp.float32)
                up_part = jnp.dot(expert_rows, up_block, preferred_element_type=jnp.float32)
                hidden = (jax.nn.silu(gate_part) * up_part).astype(jnp.bfloat16)
                partial_out = jnp.dot(hidden, down_block, preferred_element_type=jnp.float32).astype(jnp.bfloat16)
                partial_out = lax.optimization_barrier(partial_out)
                return (accum + partial_out.astype(jnp.float32), None)
            half_total, unused = lax.scan(group_step, jnp.zeros((N_EXPERT * CAPACITY, D), jnp.float32), jnp.arange(group_count, dtype=jnp.int32))
            half_total = lax.optimization_barrier(half_total.astype(jnp.bfloat16))
            total = total + half_total.astype(jnp.float32)
        return total
    expert_out = lax.map(run_expert, (buffers, jnp.arange(E, dtype=jnp.int32)))
    expert_out = expert_out.reshape(E * N_EXPERT * CAPACITY, D)
    picked = jnp.take(expert_out, row_index, axis=0) * gate_values.reshape(-1)[:, None]
    combined = lax.optimization_barrier(jnp.sum(picked.reshape(TOKENS, 2, D), axis=1))
    return (inputs + combined).astype(jnp.bfloat16)
```

```python
import jax
import jax.numpy as jnp
from jax import lax
from jax.sharding import Mesh
from jax.sharding import PartitionSpec as P

GROUP = ("dp", "tensor")
PLANE = ("dp", "tensor", "half")
CHUNKS = 2


def fold(parts, axis):
    if len(parts) != 2:
        return lax.psum_scatter(jnp.stack(parts), axis, scatter_dimension=0, tiled=False)
    low = lax.axis_index(axis) == 0
    keep = jnp.where(low, parts[0], parts[1])
    got = lax.ppermute(jnp.where(low, parts[1], parts[0]), axis, [(0, 1), (1, 0)])
    return (keep.astype(jnp.float32) + got.astype(jnp.float32)).astype(jnp.bfloat16)


def plane_sum(partial_out, share_width):
    dps, tensors, halves = (lax.axis_size(name) for name in PLANE)
    rows = partial_out.shape[0] // halves
    width = share_width // 2

    def piece(dp, tensor, half, side):
        start = (dp * tensors + tensor) * share_width + side * width
        return partial_out[half * rows : (half + 1) * rows, start : start + width]

    after = {}
    for side in range(2):
        for dp in range(dps):
            for half in range(halves):
                after[side, dp, half] = fold(
                    [piece(dp, tensor, half, side) for tensor in range(tensors)], "tensor"
                )
    left = fold(
        [fold([after[0, dp, half] for dp in range(dps)], "dp") for half in range(halves)], "half"
    )
    right = fold(
        [fold([after[1, dp, half] for half in range(halves)], "half") for dp in range(dps)], "dp"
    )
    return jnp.concatenate([left, right], axis=1)


def spread(share):
    count = lax.axis_size(GROUP)
    own = lax.axis_index(GROUP)
    got = [share]
    for step in range(1, count):
        got.append(lax.ppermute(share, GROUP, [(i, (i + step) % count) for i in range(count)]))
    got = jnp.stack(got)
    return jnp.concatenate(
        [lax.dynamic_index_in_dim(got, (own - g) % count, 0, keepdims=False) for g in range(count)],
        axis=1,
    )


def shards(tokens, norm_gain, expert_ids, gate_values, gate_weight, up_weight, down_weight):
    tok_count, feature_count = tokens.shape
    expert_count = lax.axis_size("owner")
    halves = lax.axis_size("half")
    groups = lax.axis_size("dp") * lax.axis_size("tensor")
    share_width = feature_count // groups
    capacity = tok_count * 2 // expert_count + 1
    used_rows = expert_count * capacity
    start = lax.axis_index(GROUP) * share_width

    inputs = tokens.astype(jnp.float32)
    mean_square = jnp.mean(inputs * inputs, axis=-1, keepdims=True)
    own_inputs = lax.dynamic_slice_in_dim(tokens, start, share_width, 1).astype(jnp.float32)
    own_gain = lax.dynamic_slice_in_dim(norm_gain, start, share_width, 0)
    normed = (own_inputs * lax.rsqrt(mean_square + 1e-05) * own_gain).astype(jnp.bfloat16)

    experts = jnp.arange(expert_count, dtype=jnp.int32)
    first = expert_ids[:, 0:1] == experts[None, :]
    second = expert_ids[:, 1:2] == experts[None, :]
    named = (first | second).astype(jnp.bfloat16)
    position = jnp.arange(tok_count, dtype=jnp.int32)
    earlier = (position[:, None] > position[None, :]).astype(jnp.bfloat16)
    prior = jnp.dot(earlier, named, preferred_element_type=jnp.float32).astype(jnp.int32)
    base = prior + experts[None, :] * capacity
    row_first = jnp.sum(jnp.where(first, base, 0), axis=1)
    row_second = jnp.sum(jnp.where(second, base, 0), axis=1)
    slots = jnp.arange(used_rows, dtype=jnp.int32)
    pick_first = (row_first[:, None] == slots[None, :]).astype(jnp.bfloat16)
    pick_second = (row_second[:, None] == slots[None, :]).astype(jnp.bfloat16)

    buffers = lax.dot_general(
        pick_first + pick_second, normed, (((0,), (0,)), ((), ())), preferred_element_type=jnp.float32
    ).astype(jnp.bfloat16)
    buffers = buffers.reshape(expert_count, capacity, share_width)
    bounds = [-(-capacity * i // CHUNKS) for i in range(CHUNKS + 1)]
    gathered = []
    for low, high in zip(bounds[:-1], bounds[1:]):
        used = expert_count * (high - low)
        received = lax.all_to_all(buffers[:, low:high], "owner", split_axis=0, concat_axis=0, tiled=True)
        received = jnp.pad(received.reshape(used, share_width), ((0, -used % 8), (0, 0)))
        gathered.append(lax.all_gather(received, PLANE, axis=0, tiled=True))

    returned = []
    for index, (low, high) in enumerate(zip(bounds[:-1], bounds[1:])):
        used = expert_count * (high - low)
        rows = halves * (used + -used % 8)
        source = gathered[index]
        piece_rows = jnp.concatenate(
            [source[k * rows : (k + 1) * rows] for k in range(groups)], axis=1
        )
        gate_part = jnp.dot(piece_rows, gate_weight[0], preferred_element_type=jnp.float32)
        up_part = jnp.dot(piece_rows, up_weight[0], preferred_element_type=jnp.float32)
        hidden_rows = (jax.nn.silu(gate_part) * up_part).astype(jnp.bfloat16)
        partial_out = jnp.dot(
            hidden_rows, down_weight[0], preferred_element_type=jnp.float32
        ).astype(jnp.bfloat16)
        summed = plane_sum(partial_out, share_width)
        summed = summed[:used].reshape(expert_count, high - low, share_width)
        returned.append(lax.all_to_all(summed, "owner", split_axis=0, concat_axis=0, tiled=True))
    returned = jnp.concatenate(returned, axis=1).reshape(used_rows, share_width)
    out_first = jnp.dot(pick_first, returned, preferred_element_type=jnp.float32)
    out_second = jnp.dot(pick_second, returned, preferred_element_type=jnp.float32)
    combined = out_first * gate_values[:, 0:1] + out_second * gate_values[:, 1:2]
    share_out = (own_inputs + combined).astype(jnp.bfloat16)
    return spread(share_out)


def solution(mesh):
    sizes = mesh.shape
    grid = mesh.devices.reshape(sizes["dp"], sizes["expert"] // 2, 2, sizes["tensor"])
    split = Mesh(grid, ("dp", "owner", "half", "tensor"))
    expert = ("owner", "half")
    placed = (
        P(expert, None),
        P(),
        P(expert, None),
        P(expert, None),
        P(expert, None, GROUP),
        P(expert, None, GROUP),
        P(expert, GROUP, None),
    )
    return jax.shard_map(
        shards, mesh=split, in_specs=placed, out_specs=P(expert, None), check_vma=False
    )
```
